32 devices in a mesh: scan: 2 (over y), ang: 4 (over z), row: 4 (over x, core).
Axes of the slice: x: 2, y: 2, z: 4, core: 2. Of those that a mesh axis runs over, the one named last changes fastest.
Arguments:
- raw_frames: bfloat16 [96, 128, 2560], P(('scan', 'ang'), 'row'), parts along dimension 0, may hold values from 0.099609375 to 1.5
- dark_field: bfloat16 [128, 2560], P('row'), may hold values from 0 to 0.079589844
- flat_field: bfloat16 [128, 2560], P('row'), may hold values from 0.796875 to 1.1953125
- kernel_taps: float32 [31], replicated, may hold values from 0.1 to 0.4
- partner: int32 [48], P('scan'), parts along dimension 0, may hold values from 24 to 47, as said below
- shifts: int32 [256], replicated, may hold values from -256 to 255, as said below
Outputs:
- sinograms: bfloat16 [96, 128, 2560], P('scan', ('ang', 'row')), parts along dimension 0
- correlation: float32 [256, 256], P(('scan', 'ang', 'row')), parts along dimension 0
The draws below stay inside these ranges and needn't reach their ends.
There are 2 independent parts, one for each index of `scan`. The reference program is written for one: setup_inputs(seed, part) draws one part's arguments, and reference() takes and returns one part's arrays. A program takes and returns all parts, laid end to end along the dimension named above; an argument that names none is the same for every part. Nothing has to cross between parts.
Inputs may be any that keep to these rules, and one draw needn't show every extreme that they name: partner[i] - i - 24 is -1, 0 or 1 for every i; partner[0] = 24 and partner[23] = 47. shifts[0] = -256 and shifts[255] = 255; values may repeat.
All inputs are finite; a program needn't handle non-finite values.
Results may differ from the reference program's by a relative error of at most 0.012.
The reference program's roundings to bfloat16 on the way (of `centered`, `ramp_kernel` and `mirrored`) count: a program that leaves them out, or rounds other values in their place, can miss the bound.
Values may be sent and summed in bfloat16 or wider, within the bound.
A program may use at most 128 MiB of HBM per device.

```python
import math
import jax
import jax.numpy as jnp
from jax import lax

C = 2560
TAPS = 31
SPAN = 256
NSHIFT = 256
NPROJ = 48
ROWS = 128
HALF = 24


def draw_partner(key, part):
    jitter = jax.random.randint(key, (NPROJ // 2,), -1, 2)
    position = jnp.arange(NPROJ // 2, dtype=jnp.int32)
    jitter = jnp.where(position == 0, 0, jitter)
    jitter = jnp.where(position == NPROJ // 2 - 1, 0, jitter)
    return (position + NPROJ // 2 + jitter).astype(jnp.int32)


def draw_shifts(key, part):
    values = jax.random.randint(key, (NSHIFT,), -SPAN, SPAN)
    position = jnp.arange(NSHIFT, dtype=jnp.int32)
    values = jnp.where(position == 0, -SPAN, values)
    values = jnp.where(position == NSHIFT - 1, SPAN - 1, values)
    return values.astype(jnp.int32)


def block_levels(rng, shape, cuts, smallest, largest):
    loudness, own = 1.0, jax.random.fold_in(rng, 6)
    for axis_at, blocks in cuts:
        draws = jnp.exp(jax.random.uniform(jax.random.fold_in(own, axis_at), (blocks,), jnp.float32, smallest / len(cuts), largest / len(cuts)))
        loudness = loudness * jnp.repeat(draws, shape[axis_at] // blocks).reshape([-1 if axis == axis_at else 1 for axis in range(len(shape))])
    return loudness


def setup_inputs(seed: int = 0, part: int = 0) -> dict:
    arg_keys = jax.random.split(jax.random.key(seed), 7)
    part_splits = jax.random.split(jax.random.fold_in(arg_keys[6], part), 7)
    return {
        "raw_frames": jnp.clip(0.099609375 + 1.4003906 * jax.random.uniform(part_splits[0], (NPROJ, ROWS, C), jnp.float32) ** block_levels(part_splits[0], (NPROJ, ROWS, C), ((0, 4), (1, 4)), -0.2, 0.2), 0.099609375, 1.5).astype(jnp.bfloat16),
        "dark_field": jnp.clip(0.079589844 * jax.random.uniform(arg_keys[1], (ROWS, C), jnp.float32) ** block_levels(arg_keys[1], (ROWS, C), ((0, 4),), -0.2, 0.2), 0.0, 0.079589844).astype(jnp.bfloat16),
        "flat_field": jnp.clip(0.796875 + 0.3984375 * jax.random.uniform(arg_keys[2], (ROWS, C), jnp.float32) ** block_levels(arg_keys[2], (ROWS, C), ((0, 4),), -0.2, 0.2), 0.796875, 1.1953125).astype(jnp.bfloat16),
        "kernel_taps": jnp.clip(jnp.exp(jax.random.uniform(arg_keys[3], (TAPS,), jnp.float32, math.log(0.1), math.log(0.4))), 0.1, 0.4),
        "partner": draw_partner(jax.random.fold_in(jax.random.fold_in(arg_keys[6], part), 71), part),
        "shifts": draw_shifts(jax.random.fold_in(arg_keys[6], 71), part),
    }


def absorb(raw_frames, dark_field, flat_field):
    counts = raw_frames.astype(jnp.float32)
    darkness = dark_field.astype(jnp.float32)
    brightness = flat_field.astype(jnp.float32)
    return -jnp.log((counts - darkness) / (brightness - darkness))


def column_pass(signal, kernel_taps):
    margin = kernel_taps.shape[0] // 2
    col_count = signal.shape[-1]
    padding = [(0, 0)] * (signal.ndim - 1) + [(margin, margin)]
    padded = jnp.pad(signal, padding)
    summed = kernel_taps[0] * padded[..., 0:col_count]
    for tap_index in range(1, kernel_taps.shape[0]):
        summed = summed + kernel_taps[tap_index] * padded[..., tap_index:tap_index + col_count]
    return summed


def row_pass(extended, kernel_taps, row_count, row_axis):
    summed = kernel_taps[0] * lax.slice_in_dim(extended, 0, row_count, axis=row_axis)
    for tap_index in range(1, kernel_taps.shape[0]):
        summed = summed + kernel_taps[tap_index] * lax.slice_in_dim(extended, tap_index, tap_index + row_count, axis=row_axis)
    return summed


def center_lines(lowpassed):
    return (lowpassed - jnp.mean(lowpassed, axis=-1, keepdims=True)).astype(jnp.bfloat16)


def ramp_matrix(col_count):
    distance = lax.iota(jnp.int32, col_count)[:, None] - lax.iota(jnp.int32, col_count)[None, :]
    spacing = distance.astype(jnp.float32)
    odd_distance = (distance % 2) != 0
    falloff = -4.0 / (math.pi * math.pi * jnp.maximum(spacing * spacing, 1.0))
    kernel = jnp.where(distance == 0, 1.0, jnp.where(odd_distance, falloff, 0.0))
    return kernel.astype(jnp.bfloat16)


def reference(raw_frames, dark_field, flat_field, kernel_taps, partner, shifts):
    margin = TAPS // 2
    ramp_kernel = ramp_matrix(C).astype(jnp.float32)

    def one_plane(frame_in):
        smooth = column_pass(absorb(frame_in, dark_field, flat_field), kernel_taps)
        extended = jnp.pad(smooth, ((margin, margin), (0, 0)))
        lowpassed = row_pass(extended, kernel_taps, ROWS, 0)
        centered = center_lines(lowpassed)
        filtered = jnp.dot(centered.astype(jnp.float32), ramp_kernel, precision=lax.Precision.HIGHEST)
        return centered, filtered.astype(jnp.bfloat16)

    centered, sinograms = lax.map(one_plane, raw_frames)
    factor = (HALF * C) ** -0.5

    def one_row(row_index):
        column = lax.dynamic_index_in_dim(centered, row_index, 1, False)
        leading = column[:HALF].astype(jnp.float32)
        mirrored = jnp.flip(jnp.take(column, partner, axis=0), axis=1).astype(jnp.float32)
        product = jnp.dot(leading.T, mirrored, precision=lax.Precision.HIGHEST)
        padded = jnp.pad(product, ((0, 0), (SPAN, SPAN)))
        window_width = C + 2 * SPAN
        flattened = jnp.pad(padded.reshape(-1), (0, C))
        skewed = flattened.reshape(C, window_width + 1)[:, :2 * SPAN]
        diagonal = jnp.sum(skewed, axis=0)
        return jnp.take(diagonal, shifts + SPAN) * factor

    correlation = lax.map(one_row, lax.iota(jnp.int32, ROWS))
    return sinograms, correlation
```

```python
import functools
import math

import jax
import jax.numpy as jnp
from jax import lax
from jax.experimental import pallas as pl
from jax.experimental.pallas import tpu as pltpu
from jax.sharding import PartitionSpec as P

SPAN = 256
LANES = 128
TILE = 256
MESH = pl.DeviceIdType.MESH


def split(value):
    high = value.astype(jnp.bfloat16)
    low = (value - high.astype(jnp.float32)).astype(jnp.bfloat16)
    return high, low


def band(taps_ref, lag, rows_same=None):
    tap_count = taps_ref.shape[0]
    total = jnp.zeros(lag.shape, jnp.float32)
    for tap_index in range(tap_count):
        total = jnp.where(lag == tap_index, taps_ref[tap_index], total)
    if rows_same is not None:
        total = jnp.where(rows_same, total, 0.0)
    return total


def dot(left, right):
    return jnp.dot(left, right, preferred_element_type=jnp.float32)


def filter_kernel(
    sizes,
    taps_ref,
    raw_ref,
    dark_ref,
    flat_ref,
    out_ref,
    halo_ref,
    level_ref,
    dark_ext,
    gain_ext,
    row_band,
    col_high,
    col_low,
    x_high,
    x_low,
    z_high,
    z_low,
    low_ref,
    send_ref,
    level_send,
    level_recv,
    halo_send,
    halo_recv,
    out_send,
    out_recv,
):
    ang_count, row_devices, halo, group = sizes
    planes, rows, cols = raw_ref.shape
    margin = taps_ref.shape[0] // 2
    groups = planes // group
    dests, _, share, _ = send_ref.shape
    ext = rows + 2 * halo
    scan, ang, row = lax.axis_index("scan"), lax.axis_index("ang"), lax.axis_index("row")
    has = (row > 0, row < row_devices - 1)
    peer = (jnp.maximum(row - 1, 0), jnp.minimum(row + 1, row_devices - 1))

    barrier = pltpu.get_barrier_semaphore()
    for a in range(ang_count):
        for b in range(row_devices):

            @pl.when(jnp.logical_or(ang != a, row != b))
            def _():
                pl.semaphore_signal(barrier, inc=1, device_id=(scan, a, b), device_id_type=MESH)

    pl.semaphore_wait(barrier, ang_count * row_devices - 1)

    def level_copy(side, which):
        source = (dark_ref, flat_ref)[which]
        start = 0 if side == 0 else rows - halo
        return pltpu.make_async_remote_copy(
            src_ref=source.at[pl.ds(start, halo)],
            dst_ref=level_ref.at[1 - side, which],
            send_sem=level_send.at[side, which],
            recv_sem=level_recv.at[1 - side, which],
            device_id=(scan, ang, peer[side]),
            device_id_type=MESH,
        )

    def halo_copy(side, g):
        start = 0 if side == 0 else rows - halo
        return pltpu.make_async_remote_copy(
            src_ref=raw_ref.at[pl.ds(g * group, group), pl.ds(start, halo)],
            dst_ref=halo_ref.at[1 - side, pl.ds(g * group, group)],
            send_sem=halo_send.at[side, g],
            recv_sem=halo_recv.at[1 - side, g],
            device_id=(scan, ang, peer[side]),
            device_id_type=MESH,
        )

    def start_halo(g):
        for side in range(2):

            @pl.when(has[side])
            def _():
                halo_copy(side, g).start()

    for side in range(2):

        @pl.when(has[side])
        def _():
            for which in range(2):
                level_copy(side, which).start()

    for g in range(groups):
        start_halo(g)

    out_rows = group * rows
    in_rows = group * ext
    r_out = lax.broadcasted_iota(jnp.int32, (out_rows, in_rows), 0)
    r_in = lax.broadcasted_iota(jnp.int32, (out_rows, in_rows), 1)
    lag = (r_in % ext) - (r_out % rows) - (halo - margin)
    high, low = split(band(taps_ref, lag, r_in // ext == r_out // rows))
    row_band[:out_rows] = high
    row_band[out_rows:] = low
    c_in = lax.broadcasted_iota(jnp.int32, (TILE + 2 * LANES, TILE), 0)
    c_out = lax.broadcasted_iota(jnp.int32, (TILE + 2 * LANES, TILE), 1)
    high, low = split(band(taps_ref, c_in - c_out - (LANES - margin)))
    col_high[...] = high
    col_low[...] = low
    for z_ref in (z_high, z_low):
        z_ref[:, :LANES] = jnp.zeros((out_rows, LANES), jnp.bfloat16)
        z_ref[:, LANES + cols :] = jnp.zeros((out_rows, LANES), jnp.bfloat16)

    def levels(dark, flat):
        dark = dark.astype(jnp.float32)
        return dark, jnp.log(flat.astype(jnp.float32) - dark)

    dark_ext[pl.ds(halo, rows)], gain_ext[pl.ds(halo, rows)] = levels(dark_ref[...], flat_ref[...])
    for side in range(2):

        @pl.when(has[side])
        def _():
            for which in range(2):
                level_copy(1 - side, which).wait_recv()

        at = 0 if side == 0 else halo + rows
        dark_ext[pl.ds(at, halo)], gain_ext[pl.ds(at, halo)] = levels(
            level_ref[side, 0], level_ref[side, 1]
        )

    def target(d):
        index = ang_count * row + d
        return index // row_devices, index % row_devices

    def out_copy(d, g):
        a, b = target(d)
        return pltpu.make_async_remote_copy(
            src_ref=send_ref.at[d, pl.ds(g * group, group)],
            dst_ref=out_ref.at[pl.ds(ang * planes + g * group, group)],
            send_sem=out_send.at[d, g],
            recv_sem=out_recv.at[ang, g],
            device_id=(scan, a, b),
            device_id_type=MESH,
        )

    def own_copy(d, g):
        return pltpu.make_async_copy(
            send_ref.at[d, pl.ds(g * group, group)],
            out_ref.at[pl.ds(ang * planes + g * group, group)],
            out_recv.at[ang, g],
        )

    def is_self(d):
        a, b = target(d)
        return jnp.logical_and(a == ang, b == row)

    for g in range(groups):
        for side in range(2):

            @pl.when(has[side])
            def _():
                halo_copy(1 - side, g).wait_recv()

        def absorb(p, carry):
            plane = g * group + p
            base = pl.multiple_of(p * ext, ext)

            def put(at, counts, valid):
                size = counts.shape[0]
                value = gain_ext[pl.ds(at, size)] - jnp.log(
                    counts.astype(jnp.float32) - dark_ext[pl.ds(at, size)]
                )
                if valid is not None:
                    value = jnp.where(valid, value, 0.0)
                high, low = split(value)
                x_high[pl.ds(base + at, size)] = high
                x_low[pl.ds(base + at, size)] = low

            put(0, halo_ref[0, plane], has[0])
            put(halo, raw_ref[plane], None)
            put(halo + rows, halo_ref[1, plane], has[1])
            return carry

        lax.fori_loop(0, group, absorb, 0)

        def row_pass(n, carry):
            at = pl.multiple_of(n * TILE, TILE)
            both = dot(row_band[...], x_high[:, pl.ds(at, TILE)])
            rest = dot(row_band[:out_rows], x_low[:, pl.ds(at, TILE)])
            high, low = split(both[:out_rows] + (both[out_rows:] + rest))
            to = pl.multiple_of(n * TILE + LANES, LANES)
            z_high[:, pl.ds(to, TILE)] = high
            z_low[:, pl.ds(to, TILE)] = low
            return carry

        lax.fori_loop(0, cols // TILE, row_pass, 0)

        def column_pass(n, total):
            at = pl.multiple_of(n * TILE, TILE)
            window = z_high[:, pl.ds(at, TILE + 2 * LANES)]
            rest = z_low[:, pl.ds(at, TILE + 2 * LANES)]
            value = dot(window, col_high[...]) + (
                dot(window, col_low[...]) + dot(rest, col_high[...])
            )
            low_ref[:, pl.ds(at, TILE)] = value
            return total + jnp.sum(value, axis=1, keepdims=True)

        total = lax.fori_loop(
            0, cols // TILE, column_pass, jnp.zeros((out_rows, 1), jnp.float32)
        )
        mean = total * (1.0 / cols)
        for p in range(group):
            for d in range(dests):
                at = p * rows + d * share
                send_ref[d, g * group + p] = (
                    low_ref[pl.ds(at, share)] - mean[at : at + share]
                ).astype(jnp.bfloat16)
        for d in range(dests):

            @pl.when(is_self(d))
            def _():
                own_copy(d, g).start()

            @pl.when(jnp.logical_not(is_self(d)))
            def _():
                out_copy(d, g).start()

    for g in range(groups):
        for a in range(ang_count):
            place = out_ref.at[pl.ds(a * planes + g * group, group)]
            pltpu.make_async_copy(place, place, out_recv.at[a, g]).wait()
        for d in range(dests):

            @pl.when(jnp.logical_not(is_self(d)))
            def _():
                out_copy(d, g).wait_send()

        for side in range(2):

            @pl.when(has[side])
            def _():
                halo_copy(side, g).wait_send()

    for side in range(2):

        @pl.when(has[side])
        def _():
            for which in range(2):
                level_copy(side, which).wait_send()


def filtered_lines(raw_frames, dark_field, flat_field, kernel_taps):
    planes, rows, cols = raw_frames.shape
    ang_count, row_devices = lax.axis_size("ang"), lax.axis_size("row")
    share = rows // ang_count
    margin = kernel_taps.shape[0] // 2
    halo = -(-margin // 16) * 16
    group = max(g for g in range(1, planes + 1) if planes % g == 0 and g * (rows + 2 * halo) <= 256)
    groups = planes // group
    out_rows, in_rows = group * rows, group * (rows + 2 * halo)
    vmem = pl.BlockSpec(memory_space=pltpu.VMEM)
    bf16, f32 = jnp.bfloat16, jnp.float32
    return pl.pallas_call(
        functools.partial(filter_kernel, (ang_count, row_devices, halo, group)),
        out_shape=jax.ShapeDtypeStruct((ang_count * planes, share, cols), bf16),
        in_specs=[pl.BlockSpec(memory_space=pltpu.SMEM), vmem, vmem, vmem],
        out_specs=pl.BlockSpec(memory_space=pl.ANY),
        scratch_shapes=[
            pltpu.VMEM((2, planes, halo, cols), bf16),
            pltpu.VMEM((2, 2, halo, cols), bf16),
            pltpu.VMEM((rows + 2 * halo, cols), f32),
            pltpu.VMEM((rows + 2 * halo, cols), f32),
            pltpu.VMEM((2 * out_rows, in_rows), bf16),
            pltpu.VMEM((TILE + 2 * LANES, TILE), bf16),
            pltpu.VMEM((TILE + 2 * LANES, TILE), bf16),
            pltpu.VMEM((in_rows, cols), bf16),
            pltpu.VMEM((in_rows, cols), bf16),
            pltpu.VMEM((out_rows, cols + 2 * LANES), bf16),
            pltpu.VMEM((out_rows, cols + 2 * LANES), bf16),
            pltpu.VMEM((out_rows, cols), f32),
            pltpu.VMEM((ang_count, planes, share, cols), bf16),
            pltpu.SemaphoreType.DMA((2, 2)),
            pltpu.SemaphoreType.DMA((2, 2)),
            pltpu.SemaphoreType.DMA((2, groups)),
            pltpu.SemaphoreType.DMA((2, groups)),
            pltpu.SemaphoreType.DMA((ang_count, groups)),
            pltpu.SemaphoreType.DMA((ang_count, groups)),
        ],
        compiler_params=pltpu.CompilerParams(collective_id=0, has_side_effects=True),
    )(kernel_taps, raw_frames, dark_field, flat_field)


def ramp_strip(col_count):
    tiles = col_count // TILE
    shape = ((2 * tiles - 1) * TILE, TILE)
    distance = (
        lax.broadcasted_iota(jnp.int32, shape, 0)
        - lax.broadcasted_iota(jnp.int32, shape, 1)
        - (tiles - 1) * TILE
    )
    spacing = distance.astype(jnp.float32)
    odd_distance = distance % 2 != 0
    falloff = -4.0 / (math.pi * math.pi * jnp.maximum(spacing * spacing, 1.0))
    kernel = jnp.where(distance == 0, 1.0, jnp.where(odd_distance, falloff, 0.0))
    return kernel.astype(jnp.bfloat16)


def ramp_kernel(
    share, partner_ref, shifts_ref, lines_ref, strip_ref, out_ref, corr_ref, x_ref, b_ref, prof_ref
):
    count, cols = lines_ref.shape
    half = count // share // 2
    tiles = cols // TILE
    parts = cols // LANES
    pad = SPAN // LANES
    for q in range(parts):
        x_ref[q] = lines_ref[:, pl.ds(q * LANES, LANES)].astype(jnp.float32)
    for v in range(pad):
        b_ref[v] = jnp.zeros(b_ref.shape[1:], jnp.float32)
        b_ref[pad + parts + v] = jnp.zeros(b_ref.shape[1:], jnp.float32)

    def pick(i, carry):
        source = pl.multiple_of(partner_ref[i] * share, share)
        place = pl.multiple_of(i * share, share)
        b_ref[pl.ds(pad, parts), pl.ds(place, share)] = x_ref[:, pl.ds(source, share)]
        return carry

    lax.fori_loop(0, half, pick, 0)

    def ramp(n, carry):
        start = pl.multiple_of((tiles - 1 - n) * TILE, TILE)
        value = dot(lines_ref[...], strip_ref[pl.ds(start, cols)])
        out_ref[:, pl.ds(pl.multiple_of(n * TILE, TILE), TILE)] = value.astype(jnp.bfloat16)
        return carry

    lax.fori_loop(0, tiles, ramp, 0)

    width = 2 * SPAN + LANES
    for r in range(share):
        rows = pl.ds(r, half, stride=share)
        left = jnp.concatenate(
            [x_ref[q, rows] for q in range(parts)], axis=0
        ).astype(jnp.bfloat16)
        pieces = [b_ref[v, rows] for v in range(parts + 2 * pad)]
        first = parts - 1
        right = jnp.concatenate(
            [
                jnp.concatenate([pieces[first - q + v] for q in range(parts)], axis=0)
                for v in range(width // LANES)
            ],
            axis=1,
        ).astype(jnp.bfloat16)
        product = lax.dot_general(
            left, right, (((0,), (0,)), ((), ())), preferred_element_type=jnp.float32
        )
        skewed = pltpu.roll(product, 0, 1, stride=1, stride_axis=0)
        prof_ref[pl.ds(r, 1)] = jnp.sum(skewed, axis=0, keepdims=True)[:, LANES:]

    lane = lax.broadcasted_iota(jnp.int32, (2 * SPAN, shifts_ref.shape[1]), 0)
    selector = (SPAN - 1 - lane == shifts_ref[...]).astype(jnp.float32)
    corr_ref[...] = jnp.dot(
        prof_ref[...],
        selector,
        precision=lax.Precision.HIGHEST,
        preferred_element_type=jnp.float32,
    ) * ((half * cols) ** -0.5)


def ramp_and_match(lines, partner, shifts):
    count, share, cols = lines.shape
    vmem = pl.BlockSpec(memory_space=pltpu.VMEM)
    half = count // 2
    out, corr = pl.pallas_call(
        functools.partial(ramp_kernel, share),
        out_shape=(
            jax.ShapeDtypeStruct((count * share, cols), jnp.bfloat16),
            jax.ShapeDtypeStruct((share, shifts.shape[0]), jnp.float32),
        ),
        in_specs=[pl.BlockSpec(memory_space=pltpu.SMEM), vmem, vmem, vmem],
        out_specs=(vmem, vmem),
        scratch_shapes=[
            pltpu.VMEM((cols // LANES, count * share, LANES), jnp.float32),
            pltpu.VMEM(((cols + 2 * SPAN) // LANES, half * share, LANES), jnp.float32),
            pltpu.VMEM((share, 2 * SPAN), jnp.float32),
        ],
    )(partner, shifts[None], lines.reshape(count * share, cols), ramp_strip(cols))
    return out.reshape(count, share, cols), corr


def shards(raw_frames, dark_field, flat_field, kernel_taps, partner, shifts):
    lines = filtered_lines(raw_frames, dark_field, flat_field, kernel_taps)
    return ramp_and_match(lines, partner, shifts)


def solution(mesh):
    in_specs = (
        P(("scan", "ang"), "row", None),
        P("row", None),
        P("row", None),
        P(),
        P("scan"),
        P(),
    )
    out_specs = (P("scan", ("ang", "row"), None), P(("scan", "ang", "row"), None))
    return jax.shard_map(shards, mesh=mesh, in_specs=in_specs, out_specs=out_specs, check_vma=False)
```

```python
import functools
import math

import jax
import jax.numpy as jnp
from jax import lax
from jax.experimental import pallas as pl
from jax.experimental.pallas import tpu as pltpu
from jax.sharding import PartitionSpec as P

SPAN = 256
LANES = 128
TILE = 256
CORES = 2
MESH = pl.DeviceIdType.MESH


def split(value):
    high = value.astype(jnp.bfloat16)
    low = (value - high.astype(jnp.float32)).astype(jnp.bfloat16)
    return high, low


def band(taps_ref, lag, rows_same=None):
    tap_count = taps_ref.shape[0]
    total = jnp.zeros(lag.shape, jnp.float32)
    for tap_index in range(tap_count):
        total = jnp.where(lag == tap_index, taps_ref[tap_index], total)
    if rows_same is not None:
        total = jnp.where(rows_same, total, 0.0)
    return total


def dot(left, right):
    return jnp.dot(left, right, preferred_element_type=jnp.float32)


def ramp_block(offset):
    shape = (TILE, TILE)
    distance = (
        lax.broadcasted_iota(jnp.int32, shape, 0)
        - lax.broadcasted_iota(jnp.int32, shape, 1)
        + offset
    )
    spacing = distance.astype(jnp.float32)
    odd_distance = (distance & 1) != 0
    falloff = -4.0 / (math.pi * math.pi * jnp.maximum(spacing * spacing, 1.0))
    kernel = jnp.where(distance == 0, 1.0, jnp.where(odd_distance, falloff, 0.0))
    return kernel.astype(jnp.bfloat16)


def unpack(g, planes, group, share, ang_count, lines_ref, x_ref, rows_ref):
    parts = x_ref.shape[0]
    size = group * share
    for a in range(ang_count):
        first = a * planes + g * group
        for p in range(group):
            line = lines_ref[first + p].astype(jnp.float32)
            for q in range(parts):
                x_ref[q, pl.ds((first + p) * share, share)] = line[:, q * LANES : (q + 1) * LANES]
        for q in range(parts):
            rows_ref[pl.ds(a * size, size), pl.ds(q * LANES, LANES)] = x_ref[
                q, pl.ds(first * share, size)
            ].astype(jnp.bfloat16)


def match(share, partner_ref, shifts_ref, corr_ref, x_ref, b_ref, prof_ref):
    parts, count, _ = x_ref.shape
    half = count // share // 2
    cols = parts * LANES
    pad = SPAN // LANES
    for v in range(pad):
        b_ref[v] = jnp.zeros(b_ref.shape[1:], jnp.float32)
        b_ref[pad + parts + v] = jnp.zeros(b_ref.shape[1:], jnp.float32)

    def pick(i, carry):
        offset = partner_ref[i] - i - half
        middle = half + i

        def line(index):
            return x_ref[:, pl.ds(pl.multiple_of(index * share, share), share)]

        following = line(jnp.minimum(middle + 1, 2 * half - 1))
        chosen = jnp.where(offset > 0, following, line(middle))
        place = pl.multiple_of(i * share, share)
        b_ref[pl.ds(pad, parts), pl.ds(place, share)] = jnp.where(
            offset < 0, line(middle - 1), chosen
        )
        return carry

    lax.fori_loop(0, half, pick, 0)
    width = 2 * SPAN + LANES
    for r in range(share):
        rows = pl.ds(r, half, stride=share)
        left = jnp.concatenate(
            [x_ref[q, rows] for q in range(parts)], axis=0
        ).astype(jnp.bfloat16)
        pieces = [b_ref[v, rows] for v in range(parts + 2 * pad)]
        first = parts - 1
        right = jnp.concatenate(
            [
                jnp.concatenate([pieces[first - q + v] for q in range(parts)], axis=0)
                for v in range(width // LANES)
            ],
            axis=1,
        ).astype(jnp.bfloat16)
        product = lax.dot_general(
            left, right, (((0,), (0,)), ((), ())), preferred_element_type=jnp.float32
        )
        skewed = pltpu.roll(product, 0, 1, stride=1, stride_axis=0)
        prof_ref[pl.ds(r, 1)] = jnp.sum(skewed, axis=0, keepdims=True)[:, LANES:]

    lane = lax.broadcasted_iota(jnp.int32, (2 * SPAN, shifts_ref.shape[1]), 0)
    selector = (SPAN - 1 - lane == shifts_ref[...]).astype(jnp.float32)
    corr_ref[...] = jnp.dot(
        prof_ref[...],
        selector,
        precision=lax.Precision.HIGHEST,
        preferred_element_type=jnp.float32,
    ) * ((half * cols) ** -0.5)


def filter_kernel(
    sizes,
    taps_ref,
    raw_ref,
    dark_ref,
    flat_ref,
    partner_ref,
    shifts_ref,
    out_ref,
    corr_ref,
    lines_ref,
    halo_ref,
    level_ref,
    dark_ext,
    gain_ext,
    row_band,
    col_high,
    col_low,
    x_high,
    x_low,
    z_high,
    z_low,
    low_ref,
    send_ref,
    relay_ref,
    strip_ref,
    x_ref,
    rows_ref,
    b_ref,
    prof_ref,
    level_send,
    level_recv,
    halo_send,
    halo_recv,
    out_send,
    out_recv,
    relay_send,
    relay_recv,
):
    ang_count, row_devices, halo, group = sizes
    planes, rows, cols = raw_ref.shape
    margin = taps_ref.shape[0] // 2
    groups = planes // group
    dests, _, share, _ = send_ref.shape
    ext = rows + 2 * halo
    scan, ang, row = lax.axis_index("scan"), lax.axis_index("ang"), lax.axis_index("row")
    has = (row > 0, row < row_devices - 1)
    peer = (jnp.maximum(row - 1, 0), jnp.minimum(row + 1, row_devices - 1))

    barrier = pltpu.get_barrier_semaphore()
    for a in range(ang_count):
        for b in range(row_devices):

            @pl.when(jnp.logical_or(ang != a, row != b))
            def _():
                pl.semaphore_signal(barrier, inc=1, device_id=(scan, a, b), device_id_type=MESH)

    pl.semaphore_wait(barrier, ang_count * row_devices - 1)

    def level_copy(side, which):
        source = (dark_ref, flat_ref)[which]
        start = 0 if side == 0 else rows - halo
        return pltpu.make_async_remote_copy(
            src_ref=source.at[pl.ds(start, halo)],
            dst_ref=level_ref.at[1 - side, which],
            send_sem=level_send.at[side, which],
            recv_sem=level_recv.at[1 - side, which],
            device_id=(scan, ang, peer[side]),
            device_id_type=MESH,
        )

    def halo_copy(side, g):
        start = 0 if side == 0 else rows - halo
        return pltpu.make_async_remote_copy(
            src_ref=raw_ref.at[pl.ds(g * group, group), pl.ds(start, halo)],
            dst_ref=halo_ref.at[1 - side, pl.ds(g * group, group)],
            send_sem=halo_send.at[side, g],
            recv_sem=halo_recv.at[1 - side, g],
            device_id=(scan, ang, peer[side]),
            device_id_type=MESH,
        )

    def start_halo(g):
        for side in range(2):

            @pl.when(has[side])
            def _():
                halo_copy(side, g).start()

    for side in range(2):

        @pl.when(has[side])
        def _():
            for which in range(2):
                level_copy(side, which).start()

    for g in range(groups):
        start_halo(g)

    out_rows = group * rows
    in_rows = group * ext
    r_out = lax.broadcasted_iota(jnp.int32, (out_rows, in_rows), 0)
    r_in = lax.broadcasted_iota(jnp.int32, (out_rows, in_rows), 1)
    lag = (r_in % ext) - (r_out % rows) - (halo - margin)
    high, low = split(band(taps_ref, lag, r_in // ext == r_out // rows))
    row_band[:out_rows] = high
    row_band[out_rows:] = low
    c_in = lax.broadcasted_iota(jnp.int32, (TILE + 2 * LANES, TILE), 0)
    c_out = lax.broadcasted_iota(jnp.int32, (TILE + 2 * LANES, TILE), 1)
    high, low = split(band(taps_ref, c_in - c_out - (LANES - margin)))
    col_high[...] = high
    col_low[...] = low
    for z_ref in (z_high, z_low):
        z_ref[:, :LANES] = jnp.zeros((out_rows, LANES), jnp.bfloat16)
        z_ref[:, LANES + cols :] = jnp.zeros((out_rows, LANES), jnp.bfloat16)

    def levels(dark, flat):
        dark = dark.astype(jnp.float32)
        return dark, jnp.log(flat.astype(jnp.float32) - dark)

    dark_ext[pl.ds(halo, rows)], gain_ext[pl.ds(halo, rows)] = levels(dark_ref[...], flat_ref[...])
    for side in range(2):

        @pl.when(has[side])
        def _():
            for which in range(2):
                level_copy(1 - side, which).wait_recv()

        at = 0 if side == 0 else halo + rows
        dark_ext[pl.ds(at, halo)], gain_ext[pl.ds(at, halo)] = levels(
            level_ref[side, 0], level_ref[side, 1]
        )

    upper = dests // row_devices

    def target(d):
        return upper * row + d // row_devices, d % row_devices

    def is_self(d):
        a, b = target(d)
        return jnp.logical_and(a == ang, b == row)

    def is_relayed(d):
        a, b = target(d)
        return jnp.logical_and(a != ang, b // CORES != row // CORES)

    def part(g):
        return pl.ds(g * group, group)

    def place(a, g):
        return lines_ref.at[pl.ds(a * planes + g * group, group)]

    def out_copy(d, g):
        a, b = target(d)
        return pltpu.make_async_remote_copy(
            src_ref=send_ref.at[d, part(g)],
            dst_ref=place(ang, g),
            send_sem=out_send.at[d, g],
            recv_sem=out_recv.at[ang, g],
            device_id=(scan, a, b),
            device_id_type=MESH,
        )

    def first_hop(d, g):
        return pltpu.make_async_remote_copy(
            src_ref=send_ref.at[d, part(g)],
            dst_ref=relay_ref.at[row, d // row_devices, part(g)],
            send_sem=out_send.at[d, g],
            recv_sem=relay_recv.at[row, d // row_devices, g],
            device_id=(scan, ang, d % row_devices),
            device_id_type=MESH,
        )

    def second_hop(b, u, g):
        return pltpu.make_async_remote_copy(
            src_ref=relay_ref.at[b, u, part(g)],
            dst_ref=place(ang, g),
            send_sem=relay_send.at[b, u, g],
            recv_sem=out_recv.at[ang, g],
            device_id=(scan, upper * b + u, row),
            device_id_type=MESH,
        )

    def own_copy(d, g):
        return pltpu.make_async_copy(send_ref.at[d, part(g)], place(ang, g), out_recv.at[ang, g])

    def relays(b, u):
        return jnp.logical_and(b // CORES != row // CORES, upper * b + u != ang)

    def each_relay(action):
        for b in range(row_devices):
            for u in range(upper):

                @pl.when(relays(b, u))
                def _():
                    action(b, u)

    def relay(g):
        def action(b, u):
            arrived = relay_ref.at[b, u, part(g)]
            pltpu.make_async_copy(arrived, arrived, relay_recv.at[b, u, g]).wait()
            second_hop(b, u, g).start()

        each_relay(action)

    def send(g):
        for d in range(dests):

            @pl.when(is_relayed(d))
            def _():
                first_hop(d, g).start()

        for d in range(dests):

            @pl.when(is_self(d))
            def _():
                own_copy(d, g).start()

            @pl.when(jnp.logical_not(jnp.logical_or(is_relayed(d), is_self(d))))
            def _():
                out_copy(d, g).start()

    for g in range(groups):
        for side in range(2):

            @pl.when(has[side])
            def _():
                halo_copy(1 - side, g).wait_recv()

        def absorb(p, carry):
            plane = g * group + p
            base = pl.multiple_of(p * ext, ext)

            def put(at, counts, valid):
                size = counts.shape[0]
                value = gain_ext[pl.ds(at, size)] - jnp.log(
                    counts.astype(jnp.float32) - dark_ext[pl.ds(at, size)]
                )
                if valid is not None:
                    value = jnp.where(valid, value, 0.0)
                high, low = split(value)
                x_high[pl.ds(base + at, size)] = high
                x_low[pl.ds(base + at, size)] = low

            put(0, halo_ref[0, plane], has[0])
            put(halo, raw_ref[plane], None)
            put(halo + rows, halo_ref[1, plane], has[1])
            return carry

        lax.fori_loop(0, group, absorb, 0)

        def row_pass(n, carry):
            at = pl.multiple_of(n * TILE, TILE)
            both = dot(row_band[...], x_high[:, pl.ds(at, TILE)])
            rest = dot(row_band[:out_rows], x_low[:, pl.ds(at, TILE)])
            high, low = split(both[:out_rows] + (both[out_rows:] + rest))
            to = pl.multiple_of(n * TILE + LANES, LANES)
            z_high[:, pl.ds(to, TILE)] = high
            z_low[:, pl.ds(to, TILE)] = low
            return carry

        lax.fori_loop(0, cols // TILE, row_pass, 0)

        def column_pass(n, total):
            at = pl.multiple_of(n * TILE, TILE)
            window = z_high[:, pl.ds(at, TILE + 2 * LANES)]
            rest = z_low[:, pl.ds(at, TILE + 2 * LANES)]
            value = dot(window, col_high[...]) + (
                dot(window, col_low[...]) + dot(rest, col_high[...])
            )
            low_ref[:, pl.ds(at, TILE)] = value
            return total + jnp.sum(value, axis=1, keepdims=True)

        total = lax.fori_loop(
            0, cols // TILE, column_pass, jnp.zeros((out_rows, 1), jnp.float32)
        )
        mean = total * (1.0 / cols)
        for p in range(group):
            for d in range(dests):
                at = p * rows + d * share
                send_ref[d, g * group + p] = (
                    low_ref[pl.ds(at, share)] - mean[at : at + share]
                ).astype(jnp.bfloat16)
        if g > 0:
            relay(g - 1)
        send(g)

    tiles = cols // TILE

    def build(n, carry):
        base = pl.multiple_of(n * TILE, TILE)
        strip_ref[pl.ds(base, TILE)] = ramp_block(base - (tiles - 1) * TILE)
        return carry

    lax.fori_loop(0, 2 * tiles - 1, build, 0)
    relay(groups - 1)

    size = group * share
    for g in range(groups):
        for a in range(ang_count):
            here = place(a, g)
            pltpu.make_async_copy(here, here, out_recv.at[a, g]).wait()
        unpack(g, planes, group, share, ang_count, lines_ref, x_ref, rows_ref)

        def ramp(n, carry):
            start = pl.multiple_of((tiles - 1 - n) * TILE, TILE)
            value = dot(rows_ref[...], strip_ref[pl.ds(start, cols)])
            at = pl.ds(pl.multiple_of(n * TILE, TILE), TILE)
            for a in range(ang_count):
                for p in range(group):
                    own = a * size + p * share
                    out_ref[a * planes + g * group + p, :, at] = value[own : own + share].astype(
                        jnp.bfloat16
                    )
            return carry

        lax.fori_loop(0, tiles, ramp, 0)

    match(share, partner_ref, shifts_ref, corr_ref, x_ref, b_ref, prof_ref)

    for g in range(groups):
        for d in range(dests):

            @pl.when(jnp.logical_not(is_self(d)))
            def _():
                out_copy(d, g).wait_send()

        each_relay(lambda b, u: second_hop(b, u, g).wait_send())
        for side in range(2):

            @pl.when(has[side])
            def _():
                halo_copy(side, g).wait_send()

    for side in range(2):

        @pl.when(has[side])
        def _():
            for which in range(2):
                level_copy(side, which).wait_send()


def shards(raw_frames, dark_field, flat_field, kernel_taps, partner, shifts):
    planes, rows, cols = raw_frames.shape
    ang_count, row_devices = lax.axis_size("ang"), lax.axis_size("row")
    share = rows // ang_count
    margin = kernel_taps.shape[0] // 2
    halo = -(-margin // 16) * 16
    group = max(g for g in range(1, planes + 1) if planes % g == 0 and g * (rows + 2 * halo) <= 256)
    groups = planes // group
    out_rows, in_rows = group * rows, group * (rows + 2 * halo)
    count, half = ang_count * planes, ang_count * planes // 2
    vmem = pl.BlockSpec(memory_space=pltpu.VMEM)
    smem = pl.BlockSpec(memory_space=pltpu.SMEM)
    bf16, f32 = jnp.bfloat16, jnp.float32
    return pl.pallas_call(
        functools.partial(filter_kernel, (ang_count, row_devices, halo, group)),
        out_shape=(
            jax.ShapeDtypeStruct((count, share, cols), bf16),
            jax.ShapeDtypeStruct((share, shifts.shape[0]), f32),
        ),
        in_specs=[smem, vmem, vmem, vmem, smem, vmem],
        out_specs=(vmem, vmem),
        scratch_shapes=[
            pltpu.VMEM((count, share, cols), bf16),
            pltpu.VMEM((2, planes, halo, cols), bf16),
            pltpu.VMEM((2, 2, halo, cols), bf16),
            pltpu.VMEM((rows + 2 * halo, cols), f32),
            pltpu.VMEM((rows + 2 * halo, cols), f32),
            pltpu.VMEM((2 * out_rows, in_rows), bf16),
            pltpu.VMEM((TILE + 2 * LANES, TILE), bf16),
            pltpu.VMEM((TILE + 2 * LANES, TILE), bf16),
            pltpu.VMEM((in_rows, cols), bf16),
            pltpu.VMEM((in_rows, cols), bf16),
            pltpu.VMEM((out_rows, cols + 2 * LANES), bf16),
            pltpu.VMEM((out_rows, cols + 2 * LANES), bf16),
            pltpu.VMEM((out_rows, cols), f32),
            pltpu.VMEM((ang_count, planes, share, cols), bf16),
            pltpu.VMEM((row_devices, ang_count // row_devices, planes, share, cols), bf16),
            pltpu.VMEM((2 * cols - TILE, TILE), bf16),
            pltpu.VMEM((cols // LANES, count * share, LANES), f32),
            pltpu.VMEM((ang_count * group * share, cols), bf16),
            pltpu.VMEM(((cols + 2 * SPAN) // LANES, half * share, LANES), f32),
            pltpu.VMEM((share, 2 * SPAN), f32),
            pltpu.SemaphoreType.DMA((2, 2)),
            pltpu.SemaphoreType.DMA((2, 2)),
            pltpu.SemaphoreType.DMA((2, groups)),
            pltpu.SemaphoreType.DMA((2, groups)),
            pltpu.SemaphoreType.DMA((ang_count, groups)),
            pltpu.SemaphoreType.DMA((ang_count, groups)),
            pltpu.SemaphoreType.DMA((row_devices, ang_count // row_devices, groups)),
            pltpu.SemaphoreType.DMA((row_devices, ang_count // row_devices, groups)),
        ],
        compiler_params=pltpu.CompilerParams(collective_id=0, has_side_effects=True),
    )(kernel_taps, raw_frames, dark_field, flat_field, partner, shifts[None])


def solution(mesh):
    in_specs = (
        P(("scan", "ang"), "row", None),
        P("row", None),
        P("row", None),
        P(),
        P("scan"),
        P(),
    )
    out_specs = (P("scan", ("ang", "row"), None), P(("scan", "ang", "row"), None))
    return jax.shard_map(shards, mesh=mesh, in_specs=in_specs, out_specs=out_specs, check_vma=False)
```

```python
import functools
import math

import jax
import jax.numpy as jnp
from jax import lax
from jax.experimental import pallas as pl
from jax.experimental.pallas import tpu as pltpu
from jax.sharding import PartitionSpec as P

SPAN = 256
LANES = 128
TILE = 256
CORES = 2
MESH = pl.DeviceIdType.MESH


def split(value):
    high = value.astype(jnp.bfloat16)
    low = (value - high.astype(jnp.float32)).astype(jnp.bfloat16)
    return high, low


def band(taps_ref, lag, rows_same=None):
    tap_count = taps_ref.shape[0]
    total = jnp.zeros(lag.shape, jnp.float32)
    for tap_index in range(tap_count):
        total = jnp.where(lag == tap_index, taps_ref[tap_index], total)
    if rows_same is not None:
        total = jnp.where(rows_same, total, 0.0)
    return total


def dot(left, right):
    return jnp.dot(left, right, preferred_element_type=jnp.float32)


def ramp_block(offset):
    shape = (TILE, TILE)
    distance = (
        lax.broadcasted_iota(jnp.int32, shape, 0)
        - lax.broadcasted_iota(jnp.int32, shape, 1)
        + offset
    )
    spacing = distance.astype(jnp.float32)
    odd_distance = (distance & 1) != 0
    falloff = -4.0 / (math.pi * math.pi * jnp.maximum(spacing * spacing, 1.0))
    kernel = jnp.where(distance == 0, 1.0, jnp.where(odd_distance, falloff, 0.0))
    return kernel.astype(jnp.bfloat16)


def unpack(g, planes, group, share, ang_count, lines_ref, x_ref, rows_ref):
    parts = x_ref.shape[0]
    size = group * share
    for a in range(ang_count):
        first = a * planes + g * group
        for p in range(group):
            line = lines_ref[first + p].astype(jnp.float32)
            for q in range(parts):
                x_ref[q, pl.ds((first + p) * share, share)] = line[:, q * LANES : (q + 1) * LANES]
        for q in range(parts):
            rows_ref[pl.ds(a * size, size), pl.ds(q * LANES, LANES)] = x_ref[
                q, pl.ds(first * share, size)
            ].astype(jnp.bfloat16)


def match(share, partner_ref, shifts_ref, corr_ref, x_ref, b_ref, prof_ref):
    parts, count, _ = x_ref.shape
    half = count // share // 2
    cols = parts * LANES
    pad = SPAN // LANES
    for v in range(pad):
        b_ref[v] = jnp.zeros(b_ref.shape[1:], jnp.float32)
        b_ref[pad + parts + v] = jnp.zeros(b_ref.shape[1:], jnp.float32)

    def pick(i, carry):
        offset = partner_ref[i] - i - half
        middle = half + i

        def line(index):
            return x_ref[:, pl.ds(pl.multiple_of(index * share, share), share)]

        following = line(jnp.minimum(middle + 1, 2 * half - 1))
        chosen = jnp.where(offset > 0, following, line(middle))
        place = pl.multiple_of(i * share, share)
        b_ref[pl.ds(pad, parts), pl.ds(place, share)] = jnp.where(
            offset < 0, line(middle - 1), chosen
        )
        return carry

    lax.fori_loop(0, half, pick, 0)
    width = 2 * SPAN + LANES
    for r in range(share):
        rows = pl.ds(r, half, stride=share)
        left = jnp.concatenate(
            [x_ref[q, rows] for q in range(parts)], axis=0
        ).astype(jnp.bfloat16)
        pieces = [b_ref[v, rows] for v in range(parts + 2 * pad)]
        first = parts - 1
        right = jnp.concatenate(
            [
                jnp.concatenate([pieces[first - q + v] for q in range(parts)], axis=0)
                for v in range(width // LANES)
            ],
            axis=1,
        ).astype(jnp.bfloat16)
        product = lax.dot_general(
            left, right, (((0,), (0,)), ((), ())), preferred_element_type=jnp.float32
        )
        skewed = pltpu.roll(product, 0, 1, stride=1, stride_axis=0)
        prof_ref[pl.ds(r, 1)] = jnp.sum(skewed, axis=0, keepdims=True)[:, LANES:]

    lane = lax.broadcasted_iota(jnp.int32, (2 * SPAN, shifts_ref.shape[1]), 0)
    selector = (SPAN - 1 - lane == shifts_ref[...]).astype(jnp.float32)
    corr_ref[...] = jnp.dot(
        prof_ref[...],
        selector,
        precision=lax.Precision.HIGHEST,
        preferred_element_type=jnp.float32,
    ) * ((half * cols) ** -0.5)


def filter_kernel(
    sizes,
    taps_ref,
    raw_ref,
    dark_ref,
    flat_ref,
    partner_ref,
    shifts_ref,
    out_ref,
    corr_ref,
    lines_ref,
    halo_ref,
    level_ref,
    dark_ext,
    gain_ext,
    row_band,
    col_band,
    x_high,
    x_low,
    z_high,
    z_low,
    low_ref,
    send_ref,
    relay_ref,
    strip_ref,
    x_ref,
    rows_ref,
    b_ref,
    prof_ref,
    level_send,
    level_recv,
    halo_send,
    halo_recv,
    out_send,
    out_recv,
    relay_send,
    relay_recv,
):
    ang_count, row_devices, halo, group, joined = sizes
    planes, rows, cols = raw_ref.shape
    margin = taps_ref.shape[0] // 2
    groups = planes // group
    dests, _, share, _ = send_ref.shape
    ext = rows + 2 * halo
    scan, ang, row = lax.axis_index("scan"), lax.axis_index("ang"), lax.axis_index("row")
    has = (row > 0, row < row_devices - 1)
    peer = (jnp.maximum(row - 1, 0), jnp.minimum(row + 1, row_devices - 1))

    barrier = pltpu.get_barrier_semaphore()
    for a in range(ang_count):
        for b in range(row_devices):

            @pl.when(jnp.logical_or(ang != a, row != b))
            def _():
                pl.semaphore_signal(barrier, inc=1, device_id=(scan, a, b), device_id_type=MESH)

    pl.semaphore_wait(barrier, ang_count * row_devices - 1)

    def level_copy(side, which):
        source = (dark_ref, flat_ref)[which]
        start = 0 if side == 0 else rows - halo
        return pltpu.make_async_remote_copy(
            src_ref=source.at[pl.ds(start, halo)],
            dst_ref=level_ref.at[1 - side, which],
            send_sem=level_send.at[side, which],
            recv_sem=level_recv.at[1 - side, which],
            device_id=(scan, ang, peer[side]),
            device_id_type=MESH,
        )

    def halo_copy(side, g):
        start = 0 if side == 0 else rows - halo
        return pltpu.make_async_remote_copy(
            src_ref=raw_ref.at[pl.ds(g * group, group), pl.ds(start, halo)],
            dst_ref=halo_ref.at[1 - side, pl.ds(g * group, group)],
            send_sem=halo_send.at[side, g],
            recv_sem=halo_recv.at[1 - side, g],
            device_id=(scan, ang, peer[side]),
            device_id_type=MESH,
        )

    def start_halo(g):
        for side in range(2):

            @pl.when(has[side])
            def _():
                halo_copy(side, g).start()

    for side in range(2):

        @pl.when(has[side])
        def _():
            for which in range(2):
                level_copy(side, which).start()

    for g in range(min(2, groups)):
        start_halo(g)

    out_rows = group * rows
    in_rows = group * ext
    r_out = lax.broadcasted_iota(jnp.int32, (out_rows, in_rows), 0)
    r_in = lax.broadcasted_iota(jnp.int32, (out_rows, in_rows), 1)
    lag = (r_in % ext) - (r_out % rows) - (halo - margin)
    high, low = split(band(taps_ref, lag, r_in // ext == r_out // rows))
    row_band[:out_rows] = high
    row_band[out_rows:] = low
    c_in = lax.broadcasted_iota(jnp.int32, (TILE + 2 * LANES, TILE), 0)
    c_out = lax.broadcasted_iota(jnp.int32, (TILE + 2 * LANES, TILE), 1)
    high, low = split(band(taps_ref, c_in - c_out - (LANES - margin)))
    col_band[:, :TILE] = high
    col_band[:, TILE:] = low
    for z_ref in (z_high, z_low):
        z_ref[:, :LANES] = jnp.zeros((out_rows, LANES), jnp.bfloat16)
        z_ref[:, LANES + cols :] = jnp.zeros((out_rows, LANES), jnp.bfloat16)

    def levels(dark, flat):
        dark = dark.astype(jnp.float32)
        return dark, jnp.log(flat.astype(jnp.float32) - dark)

    dark_ext[pl.ds(halo, rows)], gain_ext[pl.ds(halo, rows)] = levels(dark_ref[...], flat_ref[...])
    for side in range(2):

        @pl.when(has[side])
        def _():
            for which in range(2):
                level_copy(1 - side, which).wait_recv()

        at = 0 if side == 0 else halo + rows
        dark_ext[pl.ds(at, halo)], gain_ext[pl.ds(at, halo)] = levels(
            level_ref[side, 0], level_ref[side, 1]
        )

    upper = dests // row_devices

    def target(d):
        return upper * row + d // row_devices, d % row_devices

    def is_self(d):
        a, b = target(d)
        return jnp.logical_and(a == ang, b == row)

    def is_relayed(d):
        a, b = target(d)
        return jnp.logical_and(a != ang, b // CORES != row // CORES)

    def part(g):
        return pl.ds(g * group, group)

    def place(a, g):
        return lines_ref.at[pl.ds(a * planes + g * group, group)]

    def out_copy(d, g):
        a, b = target(d)
        return pltpu.make_async_remote_copy(
            src_ref=send_ref.at[d, part(g)],
            dst_ref=place(ang, g),
            send_sem=out_send.at[d, g],
            recv_sem=out_recv.at[ang, g],
            device_id=(scan, a, b),
            device_id_type=MESH,
        )

    def first_hop(d, g):
        return pltpu.make_async_remote_copy(
            src_ref=send_ref.at[d, part(g)],
            dst_ref=relay_ref.at[row, d // row_devices, part(g)],
            send_sem=out_send.at[d, g],
            recv_sem=relay_recv.at[row, d // row_devices, g],
            device_id=(scan, ang, d % row_devices),
            device_id_type=MESH,
        )

    def second_hop(b, u, g):
        return pltpu.make_async_remote_copy(
            src_ref=relay_ref.at[b, u, part(g)],
            dst_ref=place(ang, g),
            send_sem=relay_send.at[b, u, g],
            recv_sem=out_recv.at[ang, g],
            device_id=(scan, upper * b + u, row),
            device_id_type=MESH,
        )

    def own_copy(d, g):
        return pltpu.make_async_copy(send_ref.at[d, part(g)], place(ang, g), out_recv.at[ang, g])

    def relays(b, u):
        return jnp.logical_and(b // CORES != row // CORES, upper * b + u != ang)

    def each_relay(action):
        for b in range(row_devices):
            for u in range(upper):

                @pl.when(relays(b, u))
                def _():
                    action(b, u)

    def relay(g):
        def action(b, u):
            arrived = relay_ref.at[b, u, part(g)]
            pltpu.make_async_copy(arrived, arrived, relay_recv.at[b, u, g]).wait()
            second_hop(b, u, g).start()

        each_relay(action)

    def send(g):
        for d in range(dests):

            @pl.when(is_relayed(d))
            def _():
                first_hop(d, g).start()

        for d in range(dests):

            @pl.when(is_self(d))
            def _():
                own_copy(d, g).start()

            @pl.when(jnp.logical_not(jnp.logical_or(is_relayed(d), is_self(d))))
            def _():
                out_copy(d, g).start()

    for g in range(groups):
        for side in range(2):

            @pl.when(has[side])
            def _():
                halo_copy(1 - side, g).wait_recv()

        def absorb(p, carry):
            plane = g * group + p
            base = pl.multiple_of(p * ext, ext)

            def put(at, counts, valid):
                size = counts.shape[0]
                value = gain_ext[pl.ds(at, size)] - jnp.log(
                    counts.astype(jnp.float32) - dark_ext[pl.ds(at, size)]
                )
                if valid is not None:
                    value = jnp.where(valid, value, 0.0)
                high, low = split(value)
                x_high[pl.ds(base + at, size)] = high
                x_low[pl.ds(base + at, size)] = low

            put(0, halo_ref[0, plane], has[0])
            put(halo, raw_ref[plane], None)
            put(halo + rows, halo_ref[1, plane], has[1])
            return carry

        lax.fori_loop(0, group, absorb, 0)

        step = cols // 2 if cols // 2 % TILE == 0 else TILE

        def row_pass(n, carry):
            at = pl.multiple_of(n * step, TILE)
            both = dot(row_band[...], x_high[:, pl.ds(at, step)])
            rest = dot(row_band[:out_rows], x_low[:, pl.ds(at, step)])
            high, low = split(both[:out_rows] + (both[out_rows:] + rest))
            to = pl.multiple_of(n * step + LANES, LANES)
            z_high[:, pl.ds(to, step)] = high
            z_low[:, pl.ds(to, step)] = low
            return carry

        lax.fori_loop(0, cols // step, row_pass, 0)

        def windows(z_ref):
            return jnp.concatenate(
                [z_ref[:, n * TILE : (n + 1) * TILE + 2 * LANES] for n in range(cols // TILE)],
                axis=0,
            )

        both = dot(windows(z_high), col_band[...])
        rest = dot(windows(z_low), col_band[:, :TILE])
        value = both[:, :TILE] + (both[:, TILE:] + rest)
        total = jnp.zeros((out_rows, 1), jnp.float32)
        for n in range(cols // TILE):
            tile = value[n * out_rows : (n + 1) * out_rows]
            low_ref[:, n * TILE : (n + 1) * TILE] = tile
            total = total + jnp.sum(tile, axis=1, keepdims=True)
        mean = total * (1.0 / cols)
        for p in range(group):
            for d in range(dests):
                at = p * rows + d * share
                send_ref[d, g * group + p] = (
                    low_ref[pl.ds(at, share)] - mean[at : at + share]
                ).astype(jnp.bfloat16)
        if g > 0:
            relay(g - 1)
        send(g)
        if g + 2 < groups:
            start_halo(g + 2)

    tiles = cols // TILE

    def build(n, carry):
        base = pl.multiple_of(n * TILE, TILE)
        strip_ref[pl.ds(base, TILE)] = ramp_block(base - (tiles - 1) * TILE)
        return carry

    lax.fori_loop(0, 2 * tiles - 1, build, 0)
    relay(groups - 1)

    wide = joined * group
    size = wide * share
    for h in range(groups // joined):
        for g in range(h * joined, (h + 1) * joined):
            for a in range(ang_count):
                here = place(a, g)
                pltpu.make_async_copy(here, here, out_recv.at[a, g]).wait()
        unpack(h, planes, wide, share, ang_count, lines_ref, x_ref, rows_ref)

        def ramp(n, carry):
            start = pl.multiple_of((tiles - 1 - n) * TILE, TILE)
            value = dot(rows_ref[...], strip_ref[pl.ds(start, cols)])
            at = pl.ds(pl.multiple_of(n * TILE, TILE), TILE)
            for a in range(ang_count):
                for p in range(wide):
                    own = a * size + p * share
                    out_ref[a * planes + h * wide + p, :, at] = value[own : own + share].astype(
                        jnp.bfloat16
                    )
            return carry

        lax.fori_loop(0, tiles, ramp, 0)

    match(share, partner_ref, shifts_ref, corr_ref, x_ref, b_ref, prof_ref)

    for g in range(groups):
        for d in range(dests):

            @pl.when(jnp.logical_not(is_self(d)))
            def _():
                out_copy(d, g).wait_send()

        each_relay(lambda b, u: second_hop(b, u, g).wait_send())
        for side in range(2):

            @pl.when(has[side])
            def _():
                halo_copy(side, g).wait_send()

    for side in range(2):

        @pl.when(has[side])
        def _():
            for which in range(2):
                level_copy(side, which).wait_send()


def shards(raw_frames, dark_field, flat_field, kernel_taps, partner, shifts):
    planes, rows, cols = raw_frames.shape
    ang_count, row_devices = lax.axis_size("ang"), lax.axis_size("row")
    share = rows // ang_count
    margin = kernel_taps.shape[0] // 2
    halo = -(-margin // 16) * 16
    group = max(g for g in range(1, planes + 1) if planes % g == 0 and g * (rows + 2 * halo) <= 128)
    joined = 2 if planes // group % 2 == 0 else 1
    groups = planes // group
    out_rows, in_rows = group * rows, group * (rows + 2 * halo)
    count, half = ang_count * planes, ang_count * planes // 2
    vmem = pl.BlockSpec(memory_space=pltpu.VMEM)
    smem = pl.BlockSpec(memory_space=pltpu.SMEM)
    bf16, f32 = jnp.bfloat16, jnp.float32
    return pl.pallas_call(
        functools.partial(filter_kernel, (ang_count, row_devices, halo, group, joined)),
        out_shape=(
            jax.ShapeDtypeStruct((count, share, cols), bf16),
            jax.ShapeDtypeStruct((share, shifts.shape[0]), f32),
        ),
        in_specs=[smem, vmem, vmem, vmem, smem, vmem],
        out_specs=(vmem, vmem),
        scratch_shapes=[
            pltpu.VMEM((count, share, cols), bf16),
            pltpu.VMEM((2, planes, halo, cols), bf16),
            pltpu.VMEM((2, 2, halo, cols), bf16),
            pltpu.VMEM((rows + 2 * halo, cols), f32),
            pltpu.VMEM((rows + 2 * halo, cols), f32),
            pltpu.VMEM((2 * out_rows, in_rows), bf16),
            pltpu.VMEM((TILE + 2 * LANES, 2 * TILE), bf16),
            pltpu.VMEM((in_rows, cols), bf16),
            pltpu.VMEM((in_rows, cols), bf16),
            pltpu.VMEM((out_rows, cols + 2 * LANES), bf16),
            pltpu.VMEM((out_rows, cols + 2 * LANES), bf16),
            pltpu.VMEM((out_rows, cols), f32),
            pltpu.VMEM((ang_count, planes, share, cols), bf16),
            pltpu.VMEM((row_devices, ang_count // row_devices, planes, share, cols), bf16),
            pltpu.VMEM((2 * cols - TILE, TILE), bf16),
            pltpu.VMEM((cols // LANES, count * share, LANES), f32),
            pltpu.VMEM((ang_count * joined * group * share, cols), bf16),
            pltpu.VMEM(((cols + 2 * SPAN) // LANES, half * share, LANES), f32),
            pltpu.VMEM((share, 2 * SPAN), f32),
            pltpu.SemaphoreType.DMA((2, 2)),
            pltpu.SemaphoreType.DMA((2, 2)),
            pltpu.SemaphoreType.DMA((2, groups)),
            pltpu.SemaphoreType.DMA((2, groups)),
            pltpu.SemaphoreType.DMA((ang_count, groups)),
            pltpu.SemaphoreType.DMA((ang_count, groups)),
            pltpu.SemaphoreType.DMA((row_devices, ang_count // row_devices, groups)),
            pltpu.SemaphoreType.DMA((row_devices, ang_count // row_devices, groups)),
        ],
        compiler_params=pltpu.CompilerParams(collective_id=0, has_side_effects=True),
    )(kernel_taps, raw_frames, dark_field, flat_field, partner, shifts[None])


def solution(mesh):
    in_specs = (
        P(("scan", "ang"), "row", None),
        P("row", None),
        P("row", None),
        P(),
        P("scan"),
        P(),
    )
    out_specs = (P("scan", ("ang", "row"), None), P(("scan", "ang", "row"), None))
    return jax.shard_map(shards, mesh=mesh, in_specs=in_specs, out_specs=out_specs, check_vma=False)
```
